32 devices in a mesh: gx: 2 (over core), gy: 8 (over z, y), gz: 2 (over x).
Axes of the slice: x: 2, y: 2, z: 4, core: 2. Of those that a mesh axis runs over, the one named last changes fastest.
Arguments:
- number_densities: float32 [64, 8, 32, 256], P(None, 'gx', 'gy', 'gz'), may hold values from 0.0125 to 24, as said below
- kinetic_kelvin: float32 [8, 32, 256], P('gx', 'gy', 'gz'), may hold values from 0.5 to 3
- flow_vector: float32 [3, 8, 32, 256], P(None, 'gx', 'gy', 'gz'), may hold values from -1 to 1
- opacity_area: float32 [128, 64], replicated, may hold values from 0.0078125 to 0.078125
- illumination: float32 [6], replicated, may hold values from 0.2 to 1
- arrhenius_coefficient: float32 [128], replicated, may hold values from 0.1 to 1
- arrhenius_barrier: float32 [128], replicated, may hold values from 0.5 to 5
- exothermic_energy: float32 [256], replicated, may hold values from 0.002 to 0.02
- emission_loss: float32 [64], replicated, may hold values from 0.01 to 0.1
- participant_indices: int32 [4, 256], replicated, may hold values from 0 to 63
- demanding_patches: int32 [2, 8, 2, 4], P('gx', 'gy', 'gz'), may hold values from 0 to 16, as said below
Outputs:
- ending_populations: float32 [64, 8, 32, 256], P(None, 'gx', 'gy', 'gz')
- ending_warmth: float32 [8, 32, 256], P('gx', 'gy', 'gz')
The draws below stay inside these ranges and needn't reach their ends.
Inputs may be any that keep to these rules, and one draw needn't show every extreme that they name: `participant_indices`: stoichiometry names species. `number_densities`: densities are positive. `demanding_patches`: each brick's row holds distinct tile numbers first and 16 in its remaining slots; a brick lists at most 4 tiles and some brick lists exactly 4; the 2 bricks that share their first two brick indices together list exactly 4 tiles.
All inputs are finite; a program needn't handle non-finite values.
Results may differ from the reference program's by a relative error of at most 0.0003.
Values sent between devices are 32-bit elements; how exact they have to be, the bound alone decides.
A program may use at most 64 MiB of HBM per device.

```python
import math
from functools import partial
import jax
import jax.numpy as jnp
from jax import lax

KINDS = 64
R = 256
PHOTON_COUNT = 128
TWO = 128
NSUB = 8
BLOCK_SPAN_EAST = 4
BLOCK_SPAN_NORTH = 4
BLOCK_SPAN_UPWARD = 128
BX = 2
BY = 8
BZ = 2
MESH_SPAN_EAST = 8
MESH_SPAN_NORTH = 32
MESH_SPAN_UPWARD = 256
PATCH_COUNT = 16
MAXD = 4
N_GX = 2
N_GY = 8
N_GZ = 2


def draw_number_densities(key, part):
    base = jax.random.fold_in(key, 29)
    cell_key, line_key = jax.random.split(base, 2)
    cell_log = jax.random.uniform(cell_key, (KINDS, MESH_SPAN_EAST, MESH_SPAN_NORTH, MESH_SPAN_UPWARD), jnp.float32, jnp.log(0.1), jnp.log(3.0))
    line_log = jax.random.uniform(line_key, (KINDS, 1, MESH_SPAN_NORTH, 1), jnp.float32, jnp.log(0.125), jnp.log(8.0))
    return jnp.exp(cell_log + line_log).astype(jnp.float32)


def draw_demanding_patches(key, part):
    line_count = BX * BY
    base = jax.random.fold_in(key, 17)
    ordering_key, share_key, tile_key = jax.random.split(base, 3)
    ordering = jax.vmap(lambda sub: jax.random.permutation(sub, BZ))(jax.random.split(ordering_key, line_count))
    shares = jax.random.randint(share_key, (line_count, BZ // 2), 0, MAXD + 1)
    shares = shares.at[0, 0].set(0)
    paired = jnp.stack([MAXD - shares, shares], axis=-1).reshape(line_count, BZ)
    line_index = jnp.arange(line_count)[:, None]
    counts = jnp.zeros((line_count, BZ), jnp.int32).at[line_index, ordering].set(paired.astype(jnp.int32))
    chosen_tiles = jax.vmap(lambda sub: jax.random.permutation(sub, PATCH_COUNT)[:MAXD])(jax.random.split(tile_key, line_count * BZ))
    slot_index = jnp.arange(MAXD)[None, :]
    enumerated = jnp.where(slot_index < counts.reshape(-1, 1), chosen_tiles, PATCH_COUNT)
    return enumerated.reshape(BX, BY, BZ, MAXD).astype(jnp.int32)


def with_ends(entries, stream_key, low, high):
    index_at = [jax.random.randint(jax.random.fold_in(stream_key, axis), (), 0, length) for axis, length in enumerate(entries.shape)]
    widest = entries.shape.index(max(entries.shape))
    beside = index_at[:widest] + [(index_at[widest] + 1) % entries.shape[widest]] + index_at[widest + 1:]
    return entries.at[tuple(index_at)].set(low).at[tuple(beside)].set(high)


def shard_levels(stream_key, shape, cuts, least, high):
    loudness, own = 1.0, jax.random.fold_in(stream_key, 6)
    for position, parts in cuts:
        draws = jnp.exp(jax.random.uniform(jax.random.fold_in(own, position), (parts,), jnp.float32, least / len(cuts), high / len(cuts)))
        loudness = loudness * jnp.repeat(draws, shape[position] // parts).reshape([-1 if axis == position else 1 for axis in range(len(shape))])
    return loudness


def setup_inputs(seed: int = 0) -> dict:
    keys = jax.random.split(jax.random.key(seed), 12)
    return {
        "number_densities": draw_number_densities(jax.random.fold_in(keys[11], 71), 0),
        "kinetic_kelvin": jnp.clip(jnp.exp(math.log(3.0) - 1.7917595 * jax.random.uniform(keys[1], (MESH_SPAN_EAST, MESH_SPAN_NORTH, MESH_SPAN_UPWARD), jnp.float32) ** shard_levels(keys[1], (MESH_SPAN_EAST, MESH_SPAN_NORTH, MESH_SPAN_UPWARD), ((0, 2), (1, 8), (2, 2)), -0.2, 0.2)), 0.5, 3.0),
        "flow_vector": jnp.clip(jax.random.uniform(keys[2], (3, MESH_SPAN_EAST, MESH_SPAN_NORTH, MESH_SPAN_UPWARD), jnp.float32, -1.0, 1.0) * shard_levels(keys[2], (3, MESH_SPAN_EAST, MESH_SPAN_NORTH, MESH_SPAN_UPWARD), ((1, 2), (2, 8), (3, 2)), -0.4, 0.0), -1.0, 1.0),
        "opacity_area": jnp.clip(jnp.exp(jax.random.uniform(keys[3], (PHOTON_COUNT, KINDS), jnp.float32, math.log(0.0078125), math.log(0.078125))), 0.0078125, 0.078125),
        "illumination": jnp.clip(jnp.exp(jax.random.uniform(keys[4], (6,), jnp.float32, math.log(0.2), math.log(1.0))), 0.2, 1.0),
        "arrhenius_coefficient": jnp.clip(jnp.exp(jax.random.uniform(keys[5], (TWO,), jnp.float32, math.log(0.1), math.log(1.0))), 0.1, 1.0),
        "arrhenius_barrier": jnp.clip(jnp.exp(jax.random.uniform(keys[6], (TWO,), jnp.float32, math.log(0.5), math.log(5.0))), 0.5, 5.0),
        "exothermic_energy": jnp.clip(jnp.exp(jax.random.uniform(keys[7], (R,), jnp.float32, math.log(0.002), math.log(0.02))), 0.002, 0.02),
        "emission_loss": jnp.clip(jnp.exp(jax.random.uniform(keys[8], (KINDS,), jnp.float32, math.log(0.01), math.log(0.1))), 0.01, 0.1),
        "participant_indices": with_ends(jax.random.randint(keys[9], (4, R), 0, KINDS), jax.random.fold_in(keys[9], 1), 0, KINDS - 1).astype(jnp.int32),
        "demanding_patches": draw_demanding_patches(jax.random.fold_in(keys[11], 71), 0),
    }


HIGHEST = lax.Precision.HIGHEST
whole_update = 1.0
courant = 0.25


def reaction_tables(participant_indices):
    species = jnp.arange(KINDS, dtype=jnp.int32)[:, None]
    onehot_first = (participant_indices[0][None, :] == species).astype(jnp.float32)
    onehot_second = (participant_indices[1][None, :] == species).astype(jnp.float32)
    produced = (participant_indices[2][None, :] == species).astype(jnp.float32) + (participant_indices[3][None, :] == species).astype(jnp.float32)
    losing = jnp.concatenate([onehot_first, onehot_second[:, PHOTON_COUNT:]], axis=1)
    return produced, losing


def kinetics_advance(particle_count, voxel_warmth, photolysis_speed, lookup_arrays, participant_indices, arrhenius_coefficient, arrhenius_barrier, exothermic_energy, emission_loss, timestep_length):
    produced, losing = lookup_arrays
    reactant = jnp.take(particle_count, participant_indices[0], axis=0)
    partner = jnp.take(particle_count, participant_indices[1, PHOTON_COUNT:], axis=0)
    energetic_update = arrhenius_coefficient[:, None] * jnp.exp(-arrhenius_barrier[:, None] / voxel_warmth[None, :])
    reaction = jnp.concatenate([photolysis_speed * reactant[:PHOTON_COUNT], energetic_update * reactant[PHOTON_COUNT:] * partner], axis=0)
    removal = jnp.concatenate([photolysis_speed, energetic_update * partner, energetic_update * reactant[PHOTON_COUNT:]], axis=0)
    gained = jnp.dot(produced, reaction, precision=HIGHEST)
    loss_sum = jnp.dot(losing, removal, precision=HIGHEST)
    energy_gain = jnp.dot(exothermic_energy, reaction, precision=HIGHEST)
    energy_drain = jnp.dot(emission_loss, particle_count, precision=HIGHEST)
    new_density = (particle_count + timestep_length * gained) / (1.0 + timestep_length * loss_sum)
    updated_kelvin = (voxel_warmth + timestep_length * energy_gain) / (1.0 + timestep_length * energy_drain)
    return new_density, updated_kelvin


def advance(packed, kinetics_scheme, inner_increments):
    tile_count = packed.shape[1]
    voxels = packed.shape[2]
    cohort = math.gcd(tile_count, 16)
    grouped = packed.reshape(packed.shape[0], tile_count // cohort, cohort, voxels).transpose(1, 0, 2, 3)

    def one_group(fragment):
        particle_count = fragment[:KINDS].reshape(KINDS, -1)
        voxel_warmth = fragment[KINDS].reshape(-1)
        photolysis_speed = fragment[KINDS + 1:].reshape(PHOTON_COUNT, -1)
        for substep in range(inner_increments):
            particle_count, voxel_warmth = kinetics_advance(particle_count, voxel_warmth, photolysis_speed, *kinetics_scheme, whole_update / inner_increments)
        return particle_count.reshape(KINDS, cohort, voxels), voxel_warmth.reshape(cohort, voxels)

    group_density, group_warmth = lax.map(one_group, grouped)
    return group_density.transpose(1, 0, 2, 3).reshape(KINDS, tile_count, voxels), group_warmth.reshape(tile_count, voxels)


def line_columns(particle_count, beneath, overhead, along):
    running = jnp.cumsum(particle_count, axis=along)
    line_total = jnp.sum(particle_count, axis=along, keepdims=True)
    lower_part = beneath + (running - particle_count) + 0.5 * particle_count
    upper_part = overhead + (line_total - running) + 0.5 * particle_count
    return lower_part, upper_part


def photo_rates(columns, opacity_area, illumination, block_extents):
    summed = None
    for direction in range(6):
        optical = jnp.dot(opacity_area, columns[direction].reshape(KINDS, -1), precision=HIGHEST) / block_extents[direction // 2]
        shielded = illumination[direction] * jnp.exp(-optical)
        summed = shielded if direction == 0 else summed + shielded
    return summed


def block_contents(particle_count, voxel_warmth, block_bounds, block_extents, opacity_area, illumination, kinetics_scheme):
    columns = []
    for along in range(3):
        beneath, overhead = block_bounds[along]
        columns.extend(line_columns(particle_count, beneath, overhead, along + 1))
    photolysis_speed = photo_rates(columns, opacity_area, illumination, block_extents)
    piled_together = jnp.concatenate([particle_count.reshape(KINDS, PATCH_COUNT, -1), voxel_warmth.reshape(1, PATCH_COUNT, -1), photolysis_speed.reshape(PHOTON_COUNT, PATCH_COUNT, -1)], axis=0)
    calm_populations, calm_kelvin = advance(piled_together, kinetics_scheme, 1)
    return calm_populations, calm_kelvin, piled_together


def insert_tiles(calm_populations, calm_kelvin, enumerated, tile_density, patch_kelvin):
    particle_count = calm_populations.at[:, enumerated].set(tile_density, mode="drop")
    voxel_warmth = calm_kelvin.at[enumerated].set(patch_kelvin, mode="drop")
    return particle_count.reshape(KINDS, BLOCK_SPAN_EAST, BLOCK_SPAN_NORTH, -1), voxel_warmth.reshape(BLOCK_SPAN_EAST, BLOCK_SPAN_NORTH, -1)


def brick_offsets(number_densities, along, blocks, width):
    full_shape = number_densities.shape
    split_shape = full_shape[:along] + (blocks, width) + full_shape[along + 1:]
    totals = jnp.sum(number_densities.reshape(split_shape), axis=along + 1)
    running = jnp.cumsum(totals, axis=along)
    return running - totals, jnp.sum(totals, axis=along, keepdims=True) - running


def block_starts(*values):
    return tuple(jnp.asarray(value, jnp.int32) for value in values)


def advect_field(values, flow_vector):
    change = None
    for along in range(3):
        speed_along = flow_vector[along]
        face_speed = 0.5 * (speed_along + jnp.roll(speed_along, -1, along))
        face_flux = jnp.where(face_speed > 0,
                              face_speed * (1.5 * values - 0.5 * jnp.roll(values, 1, along)),
                              face_speed * (1.5 * jnp.roll(values, -1, along) - 0.5 * jnp.roll(values, -2, along)))
        difference = face_flux - jnp.roll(face_flux, 1, along)
        change = difference if along == 0 else change + difference
    return values - courant * change


def reference(number_densities, kinetic_kelvin, flow_vector, opacity_area, illumination, arrhenius_coefficient, arrhenius_barrier, exothermic_energy, emission_loss, participant_indices, demanding_patches):
    kinetics_scheme = (reaction_tables(participant_indices), participant_indices, arrhenius_coefficient, arrhenius_barrier, exothermic_energy, emission_loss)
    offsets_x = brick_offsets(number_densities, 1, N_GX, BLOCK_SPAN_EAST)
    offsets_y = brick_offsets(number_densities, 2, N_GY, BLOCK_SPAN_NORTH)
    offsets_z = brick_offsets(number_densities, 3, N_GZ, BLOCK_SPAN_UPWARD)
    block_extents = (float(MESH_SPAN_EAST), float(MESH_SPAN_NORTH), float(MESH_SPAN_UPWARD))
    listing = demanding_patches.reshape(-1, MAXD)
    zero = jnp.asarray(0, jnp.int32)

    def single_block(number):
        block_eastward = number // (N_GY * N_GZ)
        block_northward = (number // N_GZ) % N_GY
        block_upward = number % N_GZ
        particle_count = lax.dynamic_slice(number_densities, block_starts(zero, block_eastward * BLOCK_SPAN_EAST, block_northward * BLOCK_SPAN_NORTH, block_upward * BLOCK_SPAN_UPWARD), (KINDS, BLOCK_SPAN_EAST, BLOCK_SPAN_NORTH, BLOCK_SPAN_UPWARD))
        voxel_warmth = lax.dynamic_slice(kinetic_kelvin, block_starts(block_eastward * BLOCK_SPAN_EAST, block_northward * BLOCK_SPAN_NORTH, block_upward * BLOCK_SPAN_UPWARD), (BLOCK_SPAN_EAST, BLOCK_SPAN_NORTH, BLOCK_SPAN_UPWARD))
        start_x = block_starts(zero, block_eastward, block_northward * BLOCK_SPAN_NORTH, block_upward * BLOCK_SPAN_UPWARD)
        start_y = block_starts(zero, block_eastward * BLOCK_SPAN_EAST, block_northward, block_upward * BLOCK_SPAN_UPWARD)
        start_z = block_starts(zero, block_eastward * BLOCK_SPAN_EAST, block_northward * BLOCK_SPAN_NORTH, block_upward)
        block_bounds = (
            (lax.dynamic_slice(offsets_x[0], start_x, (KINDS, 1, BLOCK_SPAN_NORTH, BLOCK_SPAN_UPWARD)), lax.dynamic_slice(offsets_x[1], start_x, (KINDS, 1, BLOCK_SPAN_NORTH, BLOCK_SPAN_UPWARD))),
            (lax.dynamic_slice(offsets_y[0], start_y, (KINDS, BLOCK_SPAN_EAST, 1, BLOCK_SPAN_UPWARD)), lax.dynamic_slice(offsets_y[1], start_y, (KINDS, BLOCK_SPAN_EAST, 1, BLOCK_SPAN_UPWARD))),
            (lax.dynamic_slice(offsets_z[0], start_z, (KINDS, BLOCK_SPAN_EAST, BLOCK_SPAN_NORTH, 1)), lax.dynamic_slice(offsets_z[1], start_z, (KINDS, BLOCK_SPAN_EAST, BLOCK_SPAN_NORTH, 1))),
        )
        calm_populations, calm_kelvin, piled_together = block_contents(particle_count, voxel_warmth, block_bounds, block_extents, opacity_area, illumination, kinetics_scheme)
        enumerated = listing[number]
        chosen = jnp.minimum(enumerated, PATCH_COUNT - 1)
        packed = jnp.take(piled_together, chosen, axis=1)
        tile_density, patch_kelvin = advance(packed, kinetics_scheme, NSUB)
        return insert_tiles(calm_populations, calm_kelvin, enumerated, tile_density, patch_kelvin)

    block_numbers, block_warmth = lax.map(single_block, jnp.arange(N_GX * N_GY * N_GZ, dtype=jnp.int32))
    chem_abundance = block_numbers.reshape(N_GX, N_GY, N_GZ, KINDS, BLOCK_SPAN_EAST, BLOCK_SPAN_NORTH, BLOCK_SPAN_UPWARD).transpose(3, 0, 4, 1, 5, 2, 6).reshape(KINDS, MESH_SPAN_EAST, MESH_SPAN_NORTH, MESH_SPAN_UPWARD)
    ending_warmth = block_warmth.reshape(N_GX, N_GY, N_GZ, BLOCK_SPAN_EAST, BLOCK_SPAN_NORTH, BLOCK_SPAN_UPWARD).transpose(0, 3, 1, 4, 2, 5).reshape(MESH_SPAN_EAST, MESH_SPAN_NORTH, MESH_SPAN_UPWARD)
    ending_populations = lax.map(partial(advect_field, flow_vector=flow_vector), chem_abundance)
    return ending_populations, ending_warmth
```

```python
import functools

import jax
import jax.numpy as jnp
from jax import lax
from jax.experimental import pallas as pl
from jax.experimental.pallas import tpu as pltpu
from jax.sharding import PartitionSpec as P

NSUB = 8
COURANT = 0.25
MESH = pl.DeviceIdType.MESH
F32 = jnp.float32
BF16 = jnp.bfloat16


def halves(x):
    high = x.astype(BF16)
    return high, (x - high.astype(F32)).astype(BF16)


def stacked(x):
    high, low = halves(x)
    return jnp.concatenate([high, low], axis=0)


def dot(a, b):
    return jnp.dot(a, b, preferred_element_type=F32)


def kernel(
    sizes,
    extents,
    n_ref,
    t_ref,
    flow_ref,
    opacity_ref,
    coef_ref,
    barrier_ref,
    energy_ref,
    emission_ref,
    part_ref,
    illum_ref,
    patch_ref,
    out_ref,
    warm_ref,
    tiles,
    depth,
    photo,
    chem,
    acc,
    xsum,
    xother,
    zsum,
    zother,
    scan,
    scan_in,
    below,
    flow_x,
    flow_l,
    flow_r,
    flow_z,
    halo_x,
    halo_l,
    halo_r,
    zpack,
    halo_z,
    hard_n,
    hard_t,
    op_hi,
    op_lo,
    pick,
    gather_mat,
    tally_mat,
    tri,
    coef_b,
    barr_b,
    sem_first_s,
    sem_first_r,
    sem_scan_s,
    sem_scan_r,
    sem_x_s,
    sem_x_r,
    sem_l_s,
    sem_l_r,
    sem_rt_s,
    sem_rt_r,
    sem_z_s,
    sem_z_r,
):
    kinds, east, north, lanes, photons, reactions, slots, ngy, levels = sizes
    patches = east * north
    gx, gy, gz = lax.axis_index("gx"), lax.axis_index("gy"), lax.axis_index("gz")
    peer_x = (1 - gx, gy, gz)
    peer_z = (gx, gy, 1 - gz)
    left = (gx, lax.rem(gy + ngy - 1, ngy), gz)
    right = (gx, lax.rem(gy + 1, ngy), gz)
    bits = [lax.rem(gy // (1 << k), 2) for k in range(levels)]
    partners = [(gx, gy + (1 << k) * (1 - 2 * bits[k]), gz) for k in range(levels)]

    entry = pltpu.get_barrier_semaphore()
    peers = [peer_x, peer_z, left, right] + partners
    for peer in peers:
        pl.semaphore_signal(entry, inc=1, device_id=peer, device_id_type=MESH)

    def send(src, dst, ssem, rsem, to):
        return pltpu.make_async_remote_copy(
            src_ref=src,
            dst_ref=dst,
            send_sem=ssem,
            recv_sem=rsem,
            device_id=to,
            device_id_type=MESH,
        )

    lane = lax.broadcasted_iota(jnp.int32, (kinds, lanes), 1)

    xs = [None] * north
    zt = jnp.zeros((kinds, lanes), F32)
    for i in range(east):
        row = None
        for j in range(north):
            t = i * north + j
            v = n_ref[pl.ds(t, kinds, stride=patches), :]
            tiles[t] = v
            row = v if row is None else row + v
            xs[j] = v if xs[j] is None else xs[j] + v
            zt = jnp.where(lane == t, jnp.sum(v, axis=1, keepdims=True), zt)
        scan[0, i] = row
    for j in range(north):
        xsum[j] = xs[j]
    zsum[...] = zt

    pl.semaphore_wait(entry, len(peers))

    def scan_copy(k, i):
        return send(
            scan.at[k, i], scan_in.at[k, i], sem_scan_s.at[k, i], sem_scan_r.at[k, i], partners[k]
        )

    for i in range(east):
        scan_copy(0, i).start()
    first = [
        send(xsum, xother, sem_first_s.at[0], sem_first_r.at[0], peer_x),
        send(zsum, zother, sem_first_s.at[1], sem_first_r.at[1], peer_z),
        send(
            flow_ref.at[pl.ds(0, patches)], flow_x, sem_first_s.at[2], sem_first_r.at[2], peer_x
        ),
        send(
            flow_ref.at[pl.ds(patches, patches)],
            flow_r,
            sem_first_s.at[3],
            sem_first_r.at[3],
            left,
        ),
        send(
            flow_ref.at[pl.ds(patches, patches)],
            flow_l,
            sem_first_s.at[4],
            sem_first_r.at[4],
            right,
        ),
        send(
            flow_ref.at[pl.ds(2 * patches, patches)],
            flow_z,
            sem_first_s.at[5],
            sem_first_r.at[5],
            peer_z,
        ),
    ]
    for copy in first:
        copy.start()

    op = opacity_ref[...]
    op_high, op_low = halves(op)
    op_hi[...] = op_high
    lane_p = lax.broadcasted_iota(jnp.int32, op.shape, 1)
    op_lo[...] = jnp.where(lane_p < kinds, op_low.astype(F32), 0.0).astype(BF16)

    twice = lax.broadcasted_iota(jnp.int32, (2 * kinds, reactions), 0)
    twice = jnp.where(twice >= kinds, twice - kinds, twice)
    hot_a = (twice == part_ref[0:1, :]).astype(F32)
    gather_mat[0:reactions, :] = hot_a.T.astype(BF16)
    two = reactions - photons
    hot_b = (twice[:, photons:] == part_ref[1:2, photons:]).astype(F32)
    gather_mat[reactions : reactions + two, :] = hot_b.T.astype(BF16)
    extra = lax.broadcasted_iota(jnp.int32, (16, 2 * kinds), 0)
    q_high, q_low = halves(emission_ref[...])
    gather_mat[reactions + two :, :] = jnp.where(
        extra == 0, q_high.astype(F32), jnp.where(extra == 1, q_low.astype(F32), 0.0)
    ).astype(BF16)

    species = lax.broadcasted_iota(jnp.int32, (kinds, reactions), 0)
    which = lax.broadcasted_iota(jnp.int32, (kinds, reactions), 1)
    tally_mat[0:kinds, :] = (
        (species == part_ref[2:3, :]).astype(F32) + (species == part_ref[3:4, :]).astype(F32)
    ).astype(BF16)
    tally_mat[kinds : 2 * kinds, :] = (
        (species == part_ref[0:1, :]).astype(F32)
        + jnp.where(which >= photons, (species == part_ref[1:2, :]).astype(F32), 0.0)
    ).astype(BF16)
    extra = lax.broadcasted_iota(jnp.int32, (16, reactions), 0)
    e_high, e_low = halves(energy_ref[...])
    tally_mat[2 * kinds :, :] = jnp.where(
        extra == 0, e_high.astype(F32), jnp.where(extra == 1, e_low.astype(F32), 0.0)
    ).astype(BF16)

    source = lax.broadcasted_iota(jnp.int32, (2 * lanes, 2 * lanes), 0)
    source = jnp.where(source >= lanes, source - lanes, source)
    target = lax.broadcasted_iota(jnp.int32, (2 * lanes, 2 * lanes), 1)
    tri[...] = jnp.where(
        source < target, 1.0, jnp.where(source == target, 0.5, 0.0)
    ).astype(BF16)

    coef_b[...] = jnp.broadcast_to(coef_ref[...], (lanes, two)).T
    barr_b[...] = jnp.broadcast_to(-barrier_ref[...], (lanes, two)).T

    def project(x):
        s = stacked(x)
        return dot(op_hi[...], s) + dot(op_lo[...], s)

    def depth_row(i, carry):
        x = jnp.concatenate([tiles[i * north + j] for j in range(north)], axis=1)
        m = project(x)
        for j in range(north):
            depth[i * north + j] = m[:, j * lanes : (j + 1) * lanes]
        return carry

    lax.fori_loop(0, east, depth_row, 0)

    def scan_level(k):
        bit = bits[k].astype(F32)

        def chunk(i, carry):
            scan_copy(k, i).wait_recv()
            got = scan_in[k, i]
            scan[k + 1, i] = scan[k, i] + got
            if k == 0:
                below[i] = bit * got
            else:
                below[i] = below[i] + bit * got
            if k + 1 < levels:
                scan_copy(k + 1, i).start()
            return carry

        lax.fori_loop(0, east, chunk, 0)

    scan_level(0)

    first[0].wait_recv()
    high_x = gx.astype(F32)

    def x_lines(j, carry):
        other = project(xother[j])
        ms = [depth[i * north + j] for i in range(east)]
        whole = other
        for m in ms:
            whole = whole + m
        run = high_x * other
        for i in range(east):
            low = run + 0.5 * ms[i]
            up = whole - low
            photo[i * north + j] = illum_ref[0] * jnp.exp(
                low * (-1.0 / extents[0])
            ) + illum_ref[1] * jnp.exp(up * (-1.0 / extents[0]))
            run = run + ms[i]
        return carry

    lax.fori_loop(0, north, x_lines, 0)
    if levels > 1:
        scan_level(1)

    first[1].wait_recv()
    pick[...] = project(zother[...])
    high_z = gz.astype(F32)
    lane_r = lax.broadcasted_iota(jnp.int32, (photons, lanes), 1)

    def z_tile(t, carry):
        high, low_part = halves(depth[t])
        both = dot(jnp.concatenate([high, low_part], axis=1), tri[...])
        other = jnp.sum(jnp.where(lane_r == t, pick[...], 0.0), axis=1, keepdims=True)
        low = both[:, :lanes] + high_z * other
        up = both[:, lanes:] + other - low
        photo[t] = photo[t] + (
            illum_ref[4] * jnp.exp(low * (-1.0 / extents[2]))
            + illum_ref[5] * jnp.exp(up * (-1.0 / extents[2]))
        )
        return carry

    lax.fori_loop(0, patches, z_tile, 0)
    for k in range(2, levels):
        scan_level(k)

    def y_lines(i, carry):
        run = project(below[i])
        whole = project(scan[levels, i])
        for j in range(north):
            t = i * north + j
            low = run + 0.5 * depth[t]
            up = whole - low
            photo[t] = photo[t] + (
                illum_ref[2] * jnp.exp(low * (-1.0 / extents[1]))
                + illum_ref[3] * jnp.exp(up * (-1.0 / extents[1]))
            )
            run = run + depth[t]
        return carry

    lax.fori_loop(0, east, y_lines, 0)

    def react(ns, ts, ps, h):
        count = len(ns)
        g = dot(gather_mat[...], jnp.concatenate([stacked(n) for n in ns], axis=1))
        rates = []
        for q in range(count):
            c = slice(q * lanes, (q + 1) * lanes)
            speed = coef_b[...] * jnp.exp(barr_b[...] * (1.0 / ts[q]))
            rates.append(
                halves(
                    jnp.concatenate(
                        [
                            ps[q] * g[:photons, c],
                            speed * g[photons:reactions, c] * g[reactions : reactions + two, c],
                        ],
                        axis=0,
                    )
                )
            )
        pc = dot(tally_mat[...], jnp.concatenate([r[0] for r in rates], axis=1)) + dot(
            tally_mat[...], jnp.concatenate([r[1] for r in rates], axis=1)
        )
        new_n, new_t = [], []
        for q in range(count):
            c = slice(q * lanes, (q + 1) * lanes)
            n = ns[q]
            gained, used = pc[:kinds, c], pc[kinds : 2 * kinds, c]
            new_n.append((n + h * gained) * (n / (n + h * used)))
            heat = pc[2 * kinds : 2 * kinds + 1, c] + pc[2 * kinds + 1 : 2 * kinds + 2, c]
            cool = (
                g[reactions + two : reactions + two + 1, c]
                + g[reactions + two + 1 : reactions + two + 2, c]
            )
            new_t.append((ts[q] + h * heat) / (1.0 + h * cool))
        return new_n, new_t

    listed = [patch_ref[d] for d in range(slots)]
    chosen = [jnp.minimum(d, patches - 1) for d in listed]
    for d in range(slots):
        hard_n[d] = tiles[chosen[d]]
        hard_t[pl.ds(d, 1), :] = t_ref[pl.ds(chosen[d], 1), :]

    def substep(_, carry):
        ns = [hard_n[d] for d in range(slots)]
        ts = [hard_t[pl.ds(d, 1), :] for d in range(slots)]
        ps = [photo[chosen[d]] for d in range(slots)]
        ns, ts = react(ns, ts, ps, 1.0 / NSUB)
        for d in range(slots):
            hard_n[d] = ns[d]
            hard_t[pl.ds(d, 1), :] = ts[d]
        return carry

    lax.fori_loop(0, NSUB, substep, 0)

    def copy_left(i):
        return send(
            chem.at[pl.ds(i * north, 2)],
            halo_r.at[pl.ds(i * 2, 2)],
            sem_l_s.at[i],
            sem_l_r.at[i],
            left,
        )

    def copy_right(i):
        return send(
            chem.at[pl.ds(i * north + north - 2, 2)],
            halo_l.at[pl.ds(i * 2, 2)],
            sem_rt_s.at[i],
            sem_rt_r.at[i],
            right,
        )

    def copy_x(i):
        return send(
            chem.at[pl.ds(i * north, north)],
            halo_x.at[pl.ds(i * north, north)],
            sem_x_s.at[i],
            sem_x_r.at[i],
            peer_x,
        )

    def quiet_row(i, carry):
        index = [i * north + j for j in range(north)]
        ns = [tiles[t] for t in index]
        ts = [t_ref[pl.ds(t, 1), :] for t in index]
        ps = [photo[t] for t in index]
        ns, ts = react(ns, ts, ps, 1.0)
        for j in range(north):
            t = index[j]
            n, warm = ns[j], ts[j]
            for d in range(slots):
                n = jnp.where(jnp.full((kinds, lanes), listed[d] - t, jnp.int32) == 0, hard_n[d], n)
                warm = jnp.where(
                    jnp.full((1, lanes), listed[d] - t, jnp.int32) == 0,
                    hard_t[pl.ds(d, 1), :],
                    warm,
                )
            chem[t] = n
            warm_ref[pl.ds(t, 1), :] = warm
        copy_left(i).start()
        copy_right(i).start()
        copy_x(i).start()
        return carry

    lax.fori_loop(0, east, quiet_row, 0)

    packed = jnp.zeros((kinds, lanes), F32)
    for t in range(patches):
        rolled = pltpu.roll(chem[t], (4 * t + 2) % lanes, 1)
        packed = jnp.where(lane // 4 == t, rolled, packed)
    zpack[...] = packed
    zcopy = send(zpack, halo_z, sem_z_s.at[0], sem_z_r.at[0], peer_z)
    zcopy.start()

    for copy in first[2:]:
        copy.wait_recv()

    def flux(face, behind2, behind, ahead, ahead2):
        return face * jnp.where(
            face > 0, 1.5 * behind - 0.5 * behind2, 1.5 * ahead - 0.5 * ahead2
        )

    def flow_row(ref, t):
        return ref[pl.ds(t, 1), :]

    for i in range(east):
        copy_x(i).wait_recv()

    def advect_x(j, carry):
        cells = [halo_x[(east - 2) * north + j], halo_x[(east - 1) * north + j]]
        cells += [chem[i * north + j] for i in range(east)]
        cells += [halo_x[j], halo_x[north + j]]
        speed = [flow_row(flow_x, (east - 1) * north + j)]
        speed += [flow_row(flow_ref, i * north + j) for i in range(east)]
        speed += [flow_row(flow_x, j)]
        before = None
        for f in range(east + 1):
            face = jnp.broadcast_to(0.5 * (speed[f] + speed[f + 1]), (kinds, lanes))
            now = flux(face, cells[f], cells[f + 1], cells[f + 2], cells[f + 3])
            if f > 0:
                acc[(f - 1) * north + j] = now - before
            before = now
        return carry

    lax.fori_loop(0, north, advect_x, 0)

    zcopy.wait_recv()
    lane1 = lax.broadcasted_iota(jnp.int32, (1, lanes), 1)

    def roll(x, amount):
        return pltpu.roll(x, amount % lanes, 1)

    hz = halo_z[...]
    for t in range(patches):
        u = chem[t]
        b1 = jnp.where(lane == 0, roll(hz, -(4 * t + 1)), roll(u, 1))
        b2 = jnp.where(lane < 2, roll(hz, -4 * t), roll(u, 2))
        a1 = jnp.where(lane == lanes - 1, roll(hz, lanes - 1 - (4 * t + 2)), roll(u, -1))
        a2 = jnp.where(lane >= lanes - 2, roll(hz, lanes - 2 - (4 * t + 2)), roll(u, -2))
        v = flow_row(flow_ref, 2 * patches + t)
        vp = flow_row(flow_z, t)
        lower = 0.5 * (jnp.where(lane1 == 0, roll(vp, 1), roll(v, 1)) + v)
        upper = 0.5 * (v + jnp.where(lane1 == lanes - 1, roll(vp, -1), roll(v, -1)))
        lower = jnp.broadcast_to(lower, (kinds, lanes))
        upper = jnp.broadcast_to(upper, (kinds, lanes))
        acc[t] = acc[t] + (flux(upper, b1, u, a1, a2) - flux(lower, b2, b1, u, a1))

    for i in range(east):
        copy_left(i).wait_recv()
        copy_right(i).wait_recv()
        cells = [halo_l[2 * i], halo_l[2 * i + 1]]
        cells += [chem[i * north + j] for j in range(north)]
        cells += [halo_r[2 * i], halo_r[2 * i + 1]]
        speed = [flow_row(flow_l, i * north + north - 1)]
        speed += [flow_row(flow_ref, patches + i * north + j) for j in range(north)]
        speed += [flow_row(flow_r, i * north)]
        before = None
        for f in range(north + 1):
            face = jnp.broadcast_to(0.5 * (speed[f] + speed[f + 1]), (kinds, lanes))
            now = flux(face, cells[f], cells[f + 1], cells[f + 2], cells[f + 3])
            if f > 0:
                t = i * north + f - 1
                change = acc[t] + (now - before)
                out_ref[pl.ds(t, kinds, stride=patches), :] = chem[t] - COURANT * change
            before = now

    for copy in first:
        copy.wait_send()
    for k in range(levels):
        for i in range(east):
            scan_copy(k, i).wait_send()
    for i in range(east):
        copy_left(i).wait_send()
        copy_right(i).wait_send()
        copy_x(i).wait_send()
    zcopy.wait_send()


def shards(
    ngx,
    ngy,
    ngz,
    number_densities,
    kinetic_kelvin,
    flow_vector,
    opacity_area,
    illumination,
    arrhenius_coefficient,
    arrhenius_barrier,
    exothermic_energy,
    emission_loss,
    participant_indices,
    demanding_patches,
):
    kinds, east, north, lanes = number_densities.shape
    photons = opacity_area.shape[0]
    reactions = participant_indices.shape[1]
    two = reactions - photons
    slots = demanding_patches.shape[-1]
    patches = east * north
    levels = ngy.bit_length() - 1
    assert ngx == 2 and ngz == 2 and ngy == 1 << levels
    sizes = (kinds, east, north, lanes, photons, reactions, slots, ngy, levels)
    extents = (float(east * ngx), float(north * ngy), float(lanes * ngz))
    vmem = pl.BlockSpec(memory_space=pltpu.VMEM)
    smem = pl.BlockSpec(memory_space=pltpu.SMEM)
    tile = (kinds, lanes)
    DMA = pltpu.SemaphoreType.DMA
    out, warm = pl.pallas_call(
        functools.partial(kernel, sizes, extents),
        out_shape=(
            jax.ShapeDtypeStruct((kinds * patches, lanes), F32),
            jax.ShapeDtypeStruct((patches, lanes), F32),
        ),
        in_specs=[vmem] * 9 + [smem] * 2,
        out_specs=(vmem, vmem),
        scratch_shapes=[
            pltpu.VMEM((patches,) + tile, F32),
            pltpu.VMEM((patches, photons, lanes), F32),
            pltpu.VMEM((patches, photons, lanes), F32),
            pltpu.VMEM((patches,) + tile, F32),
            pltpu.VMEM((patches,) + tile, F32),
            pltpu.VMEM((north,) + tile, F32),
            pltpu.VMEM((north,) + tile, F32),
            pltpu.VMEM(tile, F32),
            pltpu.VMEM(tile, F32),
            pltpu.VMEM((levels + 1, east) + tile, F32),
            pltpu.VMEM((levels, east) + tile, F32),
            pltpu.VMEM((east,) + tile, F32),
            pltpu.VMEM((patches, lanes), F32),
            pltpu.VMEM((patches, lanes), F32),
            pltpu.VMEM((patches, lanes), F32),
            pltpu.VMEM((patches, lanes), F32),
            pltpu.VMEM((patches,) + tile, F32),
            pltpu.VMEM((2 * east,) + tile, F32),
            pltpu.VMEM((2 * east,) + tile, F32),
            pltpu.VMEM(tile, F32),
            pltpu.VMEM(tile, F32),
            pltpu.VMEM((slots,) + tile, F32),
            pltpu.VMEM((8, lanes), F32),
            pltpu.VMEM((photons, 2 * kinds), BF16),
            pltpu.VMEM((photons, 2 * kinds), BF16),
            pltpu.VMEM((photons, lanes), F32),
            pltpu.VMEM((reactions + two + 16, 2 * kinds), BF16),
            pltpu.VMEM((2 * kinds + 16, reactions), BF16),
            pltpu.VMEM((2 * lanes, 2 * lanes), BF16),
            pltpu.VMEM((two, lanes), F32),
            pltpu.VMEM((two, lanes), F32),
            DMA((6,)),
            DMA((6,)),
            DMA((levels, east)),
            DMA((levels, east)),
            DMA((east,)),
            DMA((east,)),
            DMA((east,)),
            DMA((east,)),
            DMA((east,)),
            DMA((east,)),
            DMA((1,)),
            DMA((1,)),
        ],
        compiler_params=pltpu.CompilerParams(
            collective_id=0, has_side_effects=True, vmem_limit_bytes=48 << 20
        ),
    )(
        number_densities.reshape(kinds * patches, lanes),
        kinetic_kelvin.reshape(patches, lanes),
        flow_vector.reshape(3 * patches, lanes),
        jnp.concatenate([opacity_area, opacity_area], axis=1),
        arrhenius_coefficient.reshape(1, two),
        arrhenius_barrier.reshape(1, two),
        exothermic_energy.reshape(1, reactions),
        jnp.concatenate([emission_loss, emission_loss]).reshape(1, 2 * kinds),
        participant_indices,
        illumination,
        demanding_patches.reshape(slots),
    )
    return out.reshape(number_densities.shape), warm.reshape(kinetic_kelvin.shape)


def solution(mesh):
    cells = P(None, "gx", "gy", "gz")
    return jax.shard_map(
        functools.partial(shards, mesh.shape["gx"], mesh.shape["gy"], mesh.shape["gz"]),
        mesh=mesh,
        in_specs=(
            cells,
            P("gx", "gy", "gz"),
            cells,
            P(),
            P(),
            P(),
            P(),
            P(),
            P(),
            P(),
            P("gx", "gy", "gz", None),
        ),
        out_specs=(cells, P("gx", "gy", "gz")),
        check_vma=False,
    )
```

```python
import functools

import jax
import jax.numpy as jnp
from jax import lax
from jax.experimental import pallas as pl
from jax.experimental.pallas import tpu as pltpu
from jax.sharding import PartitionSpec as P

NSUB = 8
COURANT = 0.25
MESH = pl.DeviceIdType.MESH
F32 = jnp.float32
BF16 = jnp.bfloat16


def halves(x):
    high = x.astype(BF16)
    return high, (x - high.astype(F32)).astype(BF16)


def stacked(x):
    high, low = halves(x)
    return jnp.concatenate([high, low], axis=0)


def dot(a, b):
    return jnp.dot(a, b, preferred_element_type=F32)


def kernel(
    sizes,
    extents,
    n_any,
    t_ref,
    flow_ref,
    opacity_ref,
    coef_ref,
    barrier_ref,
    energy_ref,
    emission_ref,
    part_ref,
    illum_ref,
    patch_ref,
    out_ref,
    warm_ref,
    n_ref,
    tiles,
    depth,
    photo,
    chem,
    acc,
    xsum,
    xother,
    zsum,
    zother,
    scan,
    scan_in,
    below,
    above,
    ey_low,
    ey_up,
    first_a,
    first_pc,
    first_cool,
    flow_x,
    flow_l,
    flow_r,
    flow_z,
    halo_x,
    halo_l,
    halo_r,
    zpack,
    halo_z,
    hard_n,
    hard_t,
    op_hi,
    op_lo,
    pick,
    gather_mat,
    tally_p,
    tally_t,
    tri,
    coef_b,
    barr_b,
    sem_n,
    sem_first_s,
    sem_first_r,
    sem_scan_s,
    sem_scan_r,
    sem_x_s,
    sem_x_r,
    sem_l_s,
    sem_l_r,
    sem_rt_s,
    sem_rt_r,
    sem_z_s,
    sem_z_r,
):
    kinds, east, north, lanes, photons, reactions, slots, ngy, levels = sizes
    patches = east * north
    gx, gy, gz = lax.axis_index("gx"), lax.axis_index("gy"), lax.axis_index("gz")
    peer_x = (1 - gx, gy, gz)
    peer_z = (gx, gy, 1 - gz)
    left = (gx, lax.rem(gy + ngy - 1, ngy), gz)
    right = (gx, lax.rem(gy + 1, ngy), gz)
    bits = [lax.rem(gy // (1 << k), 2) for k in range(levels)]
    partners = [(gx, gy + (1 << k) * (1 - 2 * bits[k]), gz) for k in range(levels)]

    entry = pltpu.get_barrier_semaphore()
    peers = [peer_x, peer_z] + partners
    for peer in peers:
        pl.semaphore_signal(entry, inc=1, device_id=peer, device_id_type=MESH)

    def send(src, dst, ssem, rsem, to):
        return pltpu.make_async_remote_copy(
            src_ref=src,
            dst_ref=dst,
            send_sem=ssem,
            recv_sem=rsem,
            device_id=to,
            device_id_type=MESH,
        )

    lane = lax.broadcasted_iota(jnp.int32, (kinds, lanes), 1)

    n_copy = pltpu.make_async_copy(n_any, n_ref, sem_n.at[0])
    n_copy.start()

    op = opacity_ref[...].T
    op = jnp.concatenate([op, op], axis=1)
    op_high, op_low = halves(op)
    op_hi[...] = op_high
    lane_p = lax.broadcasted_iota(jnp.int32, op.shape, 1)
    op_lo[...] = jnp.where(lane_p < kinds, op_low.astype(F32), 0.0).astype(BF16)

    twice = lax.broadcasted_iota(jnp.int32, (2 * kinds, reactions), 0)
    twice = jnp.where(twice >= kinds, twice - kinds, twice)
    hot_a = (twice == part_ref[0:1, :]).astype(F32)
    gather_mat[0:reactions, :] = hot_a.T.astype(BF16)
    two = reactions - photons
    hot_b = (twice[:, photons:] == part_ref[1:2, photons:]).astype(F32)
    gather_mat[reactions : reactions + two, :] = hot_b.T.astype(BF16)
    extra = lax.broadcasted_iota(jnp.int32, (16, 2 * kinds), 0)
    q_high, q_low = halves(emission_ref[...])
    gather_mat[reactions + two :, :] = jnp.where(
        extra == 0, q_high.astype(F32), jnp.where(extra == 1, q_low.astype(F32), 0.0)
    ).astype(BF16)

    species = lax.broadcasted_iota(jnp.int32, (kinds, reactions), 0)
    which = lax.broadcasted_iota(jnp.int32, (kinds, reactions), 1)
    made = (species == part_ref[2:3, :]).astype(F32) + (species == part_ref[3:4, :]).astype(F32)
    used_up = (species == part_ref[0:1, :]).astype(F32) + jnp.where(
        which >= photons, (species == part_ref[1:2, :]).astype(F32), 0.0
    )
    extra = lax.broadcasted_iota(jnp.int32, (16, reactions), 0)
    e_high, e_low = halves(energy_ref[...])
    heats = jnp.where(
        extra == 0, e_high.astype(F32), jnp.where(extra == 1, e_low.astype(F32), 0.0)
    )
    tally = jnp.concatenate([made, used_up, heats], axis=0)
    tally_p[...] = jnp.concatenate([tally[:, :photons]] * 2, axis=1).astype(BF16)
    tally_t[...] = jnp.concatenate([tally[:, photons:]] * 2, axis=1).astype(BF16)

    source = lax.broadcasted_iota(jnp.int32, (2 * lanes, 2 * lanes), 0)
    source = jnp.where(source >= lanes, source - lanes, source)
    target = lax.broadcasted_iota(jnp.int32, (2 * lanes, 2 * lanes), 1)
    tri[...] = jnp.where(
        source < target, 1.0, jnp.where(source == target, 0.5, 0.0)
    ).astype(BF16)

    coef_b[...] = jnp.broadcast_to(coef_ref[...], (lanes, two)).T
    barr_b[...] = jnp.broadcast_to(-barrier_ref[...], (lanes, two)).T

    n_copy.wait()
    xs = [None] * north
    zt = jnp.zeros((kinds, lanes), F32)
    for i in range(east):
        row = None
        for j in range(north):
            t = i * north + j
            v = n_ref[pl.ds(t, kinds, stride=patches), :]
            tiles[t] = v
            row = v if row is None else row + v
            xs[j] = v if xs[j] is None else xs[j] + v
            zt = jnp.where(lane == t, jnp.sum(v, axis=1, keepdims=True), zt)
        scan[0, i] = row
    for j in range(north):
        xsum[j] = xs[j]
    zsum[...] = zt

    pl.semaphore_wait(entry, len(peers))

    def scan_copy(k, i):
        return send(
            scan.at[k, i], scan_in.at[k, i], sem_scan_s.at[k, i], sem_scan_r.at[k, i], partners[k]
        )

    for i in range(east):
        scan_copy(0, i).start()
    first = [
        send(xsum, xother, sem_first_s.at[0], sem_first_r.at[0], peer_x),
        send(zsum, zother, sem_first_s.at[1], sem_first_r.at[1], peer_z),
        send(
            flow_ref.at[pl.ds(0, patches)], flow_x, sem_first_s.at[2], sem_first_r.at[2], peer_x
        ),
        send(
            flow_ref.at[pl.ds(2 * patches, patches)],
            flow_z,
            sem_first_s.at[5],
            sem_first_r.at[5],
            peer_z,
        ),
    ]
    for copy in first:
        copy.start()

    def project(x):
        s = stacked(x)
        return dot(op_hi[...], s) + dot(op_lo[...], s)

    def depth_row(i, carry):
        x = jnp.concatenate([tiles[i * north + j] for j in range(north)], axis=1)
        m = project(x)
        for j in range(north):
            depth[i * north + j] = m[:, j * lanes : (j + 1) * lanes]
        return carry

    lax.fori_loop(0, east, depth_row, 0)

    def scan_step(k, i):
        bit = bits[k].astype(F32)
        scan_copy(k, i).wait_recv()
        got = scan_in[k, i]
        if k + 1 < levels:
            scan[k + 1, i] = scan[k, i] + got
            scan_copy(k + 1, i).start()
        if k == 0:
            below[i] = bit * got
            above[i] = (1.0 - bit) * got
        else:
            below[i] = below[i] + bit * got
            above[i] = above[i] + (1.0 - bit) * got

    def y_lines(i, carry):
        ms = [depth[i * north + j] for j in range(north)]
        whole = ms[0]
        for m in ms[1:]:
            whole = whole + m
        run = None
        for j in range(north):
            low = 0.5 * ms[j] if run is None else run + 0.5 * ms[j]
            t = i * north + j
            ey_low[t] = illum_ref[2] * jnp.exp(low * (-1.0 / extents[1]))
            ey_up[t] = illum_ref[3] * jnp.exp((whole - low) * (-1.0 / extents[1]))
            run = ms[j] if run is None else run + ms[j]
        return carry

    high_x = gx.astype(F32)

    def x_lines(j, carry):
        other = project(xother[j])
        ms = [depth[i * north + j] for i in range(east)]
        whole = other
        for m in ms:
            whole = whole + m
        run = high_x * other
        for i in range(east):
            low = run + 0.5 * ms[i]
            up = whole - low
            photo[i * north + j] = illum_ref[0] * jnp.exp(
                low * (-1.0 / extents[0])
            ) + illum_ref[1] * jnp.exp(up * (-1.0 / extents[0]))
            run = run + ms[i]
        return carry

    high_z = gz.astype(F32)

    def z_row(i):
        parts = []
        for j in range(north):
            high, low_part = halves(depth[i * north + j])
            parts.append(jnp.concatenate([high, low_part], axis=1))
        both = dot(jnp.concatenate(parts, axis=0), tri[...])
        for j in range(north):
            t = i * north + j
            other = pick[:, t : t + 1]
            rows = slice(j * photons, (j + 1) * photons)
            low = both[rows, :lanes] + high_z * other
            up = both[rows, lanes:] + other - low
            photo[t] = photo[t] + (
                illum_ref[4] * jnp.exp(low * (-1.0 / extents[2]))
                + illum_ref[5] * jnp.exp(up * (-1.0 / extents[2]))
            )

    def two_body(ns, ts):
        g = dot(gather_mat[...], jnp.concatenate([stacked(n) for n in ns], axis=1))
        rates = []
        for q in range(len(ns)):
            c = slice(q * lanes, (q + 1) * lanes)
            speed = coef_b[...] * jnp.exp(barr_b[...] * (1.0 / ts[q]))
            rates.append(
                stacked(speed * g[photons:reactions, c] * g[reactions : reactions + two, c])
            )
        pc = dot(tally_t[...], jnp.concatenate(rates, axis=1))
        result = []
        for q in range(len(ns)):
            c = slice(q * lanes, (q + 1) * lanes)
            cool = (
                g[reactions + two : reactions + two + 1, c]
                + g[reactions + two + 1 : reactions + two + 2, c]
            )
            result.append((g[:photons, c], pc[:, c], cool))
        return result

    def finish(ns, ts, ps, halfway, h):
        rates = [stacked(p * half[0]) for p, half in zip(ps, halfway)]
        pc_all = dot(tally_p[...], jnp.concatenate(rates, axis=1))
        new_n, new_t = [], []
        for q in range(len(ns)):
            c = slice(q * lanes, (q + 1) * lanes)
            n = ns[q]
            pc = pc_all[:, c] + halfway[q][1]
            gained, used = pc[:kinds], pc[kinds : 2 * kinds]
            new_n.append((n + h * gained) * (n / (n + h * used)))
            heat = pc[2 * kinds : 2 * kinds + 1] + pc[2 * kinds + 1 : 2 * kinds + 2]
            new_t.append((ts[q] + h * heat) / (1.0 + h * halfway[q][2]))
        return new_n, new_t

    def first_row(i, carry):
        index = [i * north + j for j in range(north)]
        found = two_body([tiles[t] for t in index], [t_ref[pl.ds(t, 1), :] for t in index])
        for t, (a, pc, cool) in zip(index, found):
            first_a[t] = a
            first_pc[t] = pc
            first_cool[pl.ds(t, 1), :] = cool
        return carry

    def x_part():
        first[0].wait_recv()
        lax.fori_loop(0, north, x_lines, 0)
        first[1].wait_recv()
        pick[...] = project(zother[...])

    pieces = [
        lambda: lax.fori_loop(0, east, y_lines, 0),
        x_part,
        lambda: lax.fori_loop(0, east, first_row, 0),
    ] + [functools.partial(z_row, i) for i in range(east)]
    stages = levels + east - 1
    for stage in range(stages):
        if stage < len(pieces):
            pieces[stage]()
        for k in range(levels - 1, -1, -1):
            if 0 <= stage - k < east:
                if stage == stages - 1 and k == levels - 1:
                    for piece in pieces[stages:]:
                        piece()
                scan_step(k, stage - k)

    flow_y = [
        send(
            flow_ref.at[pl.ds(patches, patches)],
            flow_r,
            sem_first_s.at[3],
            sem_first_r.at[3],
            left,
        ),
        send(
            flow_ref.at[pl.ds(patches, patches)],
            flow_l,
            sem_first_s.at[4],
            sem_first_r.at[4],
            right,
        ),
    ]
    for copy in flow_y:
        copy.start()

    def y_join(i, carry):
        low = jnp.exp(project(below[i]) * (-1.0 / extents[1]))
        up = jnp.exp(project(above[i]) * (-1.0 / extents[1]))
        for j in range(north):
            t = i * north + j
            photo[t] = photo[t] + (ey_low[t] * low + ey_up[t] * up)
        return carry

    lax.fori_loop(0, east, y_join, 0)

    listed = [patch_ref[d] for d in range(slots)]
    chosen = [jnp.minimum(d, patches - 1) for d in listed]
    hard_p = lambda: [photo[chosen[d]] for d in range(slots)]

    def keep(ns, ts):
        for d in range(slots):
            hard_n[d] = ns[d]
            hard_t[pl.ds(d, 1), :] = ts[d]

    keep(
        *finish(
            [tiles[t] for t in chosen],
            [t_ref[pl.ds(t, 1), :] for t in chosen],
            hard_p(),
            [(first_a[t], first_pc[t], first_cool[pl.ds(t, 1), :]) for t in chosen],
            1.0 / NSUB,
        )
    )

    def substep(_, carry):
        ns = [hard_n[d] for d in range(slots)]
        ts = [hard_t[pl.ds(d, 1), :] for d in range(slots)]
        keep(*finish(ns, ts, hard_p(), two_body(ns, ts), 1.0 / NSUB))
        return carry

    lax.fori_loop(1, NSUB, substep, 0)

    def copy_left(i):
        return send(
            chem.at[pl.ds(i * north, 2)],
            halo_r.at[pl.ds(i * 2, 2)],
            sem_l_s.at[i],
            sem_l_r.at[i],
            left,
        )

    def copy_right(i):
        return send(
            chem.at[pl.ds(i * north + north - 2, 2)],
            halo_l.at[pl.ds(i * 2, 2)],
            sem_rt_s.at[i],
            sem_rt_r.at[i],
            right,
        )

    def copy_x(i):
        return send(
            chem.at[pl.ds(i * north, north)],
            halo_x.at[pl.ds(i * north, north)],
            sem_x_s.at[i],
            sem_x_r.at[i],
            peer_x,
        )

    def quiet_row(i, carry):
        index = [i * north + j for j in range(north)]
        ns = [tiles[t] for t in index]
        ts = [t_ref[pl.ds(t, 1), :] for t in index]
        ps = [photo[t] for t in index]
        halfway = [(first_a[t], first_pc[t], first_cool[pl.ds(t, 1), :]) for t in index]
        ns, ts = finish(ns, ts, ps, halfway, 1.0)
        for j in range(north):
            t = index[j]
            n, warm = ns[j], ts[j]
            for d in range(slots):
                n = jnp.where(jnp.full((kinds, lanes), listed[d] - t, jnp.int32) == 0, hard_n[d], n)
                warm = jnp.where(
                    jnp.full((1, lanes), listed[d] - t, jnp.int32) == 0,
                    hard_t[pl.ds(d, 1), :],
                    warm,
                )
            chem[t] = n
            warm_ref[pl.ds(t, 1), :] = warm
        copy_left(i).start()
        copy_right(i).start()
        copy_x(i).start()
        return carry

    lax.fori_loop(0, east, quiet_row, 0)

    packed = jnp.zeros((kinds, lanes), F32)
    for t in range(patches):
        rolled = pltpu.roll(chem[t], (4 * t + 2) % lanes, 1)
        packed = jnp.where(lane // 4 == t, rolled, packed)
    zpack[...] = packed
    zcopy = send(zpack, halo_z, sem_z_s.at[0], sem_z_r.at[0], peer_z)
    zcopy.start()

    for copy in first[2:] + flow_y:
        copy.wait_recv()

    def flux(face, behind2, behind, ahead, ahead2):
        return face * jnp.where(
            face > 0, 1.5 * behind - 0.5 * behind2, 1.5 * ahead - 0.5 * ahead2
        )

    def flow_row(ref, t):
        return ref[pl.ds(t, 1), :]

    for i in range(east):
        copy_x(i).wait_recv()

    def advect_x(j, carry):
        cells = [halo_x[(east - 2) * north + j], halo_x[(east - 1) * north + j]]
        cells += [chem[i * north + j] for i in range(east)]
        cells += [halo_x[j], halo_x[north + j]]
        speed = [flow_row(flow_x, (east - 1) * north + j)]
        speed += [flow_row(flow_ref, i * north + j) for i in range(east)]
        speed += [flow_row(flow_x, j)]
        before = None
        for f in range(east + 1):
            face = jnp.broadcast_to(0.5 * (speed[f] + speed[f + 1]), (kinds, lanes))
            now = flux(face, cells[f], cells[f + 1], cells[f + 2], cells[f + 3])
            if f > 0:
                acc[(f - 1) * north + j] = now - before
            before = now
        return carry

    lax.fori_loop(0, north, advect_x, 0)

    zcopy.wait_recv()
    lane1 = lax.broadcasted_iota(jnp.int32, (1, lanes), 1)

    def roll(x, amount):
        return pltpu.roll(x, amount % lanes, 1)

    hz = halo_z[...]
    for t in range(patches):
        u = chem[t]
        b1 = jnp.where(lane == 0, roll(hz, -(4 * t + 1)), roll(u, 1))
        b2 = jnp.where(lane < 2, roll(hz, -4 * t), roll(u, 2))
        a1 = jnp.where(lane == lanes - 1, roll(hz, lanes - 1 - (4 * t + 2)), roll(u, -1))
        a2 = jnp.where(lane >= lanes - 2, roll(hz, lanes - 2 - (4 * t + 2)), roll(u, -2))
        v = flow_row(flow_ref, 2 * patches + t)
        vp = flow_row(flow_z, t)
        lower = 0.5 * (jnp.where(lane1 == 0, roll(vp, 1), roll(v, 1)) + v)
        upper = 0.5 * (v + jnp.where(lane1 == lanes - 1, roll(vp, -1), roll(v, -1)))
        lower = jnp.broadcast_to(lower, (kinds, lanes))
        upper = jnp.broadcast_to(upper, (kinds, lanes))
        acc[t] = acc[t] + (flux(upper, b1, u, a1, a2) - flux(lower, b2, b1, u, a1))

    for i in range(east):
        copy_left(i).wait_recv()
        copy_right(i).wait_recv()
        cells = [halo_l[2 * i], halo_l[2 * i + 1]]
        cells += [chem[i * north + j] for j in range(north)]
        cells += [halo_r[2 * i], halo_r[2 * i + 1]]
        speed = [flow_row(flow_l, i * north + north - 1)]
        speed += [flow_row(flow_ref, patches + i * north + j) for j in range(north)]
        speed += [flow_row(flow_r, i * north)]
        before = None
        for f in range(north + 1):
            face = jnp.broadcast_to(0.5 * (speed[f] + speed[f + 1]), (kinds, lanes))
            now = flux(face, cells[f], cells[f + 1], cells[f + 2], cells[f + 3])
            if f > 0:
                t = i * north + f - 1
                change = acc[t] + (now - before)
                out_ref[pl.ds(t, kinds, stride=patches), :] = chem[t] - COURANT * change
            before = now

    for copy in first + flow_y:
        copy.wait_send()
    for k in range(levels):
        for i in range(east):
            scan_copy(k, i).wait_send()
    for i in range(east):
        copy_left(i).wait_send()
        copy_right(i).wait_send()
        copy_x(i).wait_send()
    zcopy.wait_send()


def shards(
    ngx,
    ngy,
    ngz,
    number_densities,
    kinetic_kelvin,
    flow_vector,
    opacity_area,
    illumination,
    arrhenius_coefficient,
    arrhenius_barrier,
    exothermic_energy,
    emission_loss,
    participant_indices,
    demanding_patches,
):
    kinds, east, north, lanes = number_densities.shape
    photons = opacity_area.shape[0]
    reactions = participant_indices.shape[1]
    two = reactions - photons
    slots = demanding_patches.shape[-1]
    patches = east * north
    levels = ngy.bit_length() - 1
    assert ngx == 2 and ngz == 2 and ngy == 1 << levels
    sizes = (kinds, east, north, lanes, photons, reactions, slots, ngy, levels)
    extents = (float(east * ngx), float(north * ngy), float(lanes * ngz))
    vmem = pl.BlockSpec(memory_space=pltpu.VMEM)
    smem = pl.BlockSpec(memory_space=pltpu.SMEM)
    tile = (kinds, lanes)
    DMA = pltpu.SemaphoreType.DMA
    out, warm = pl.pallas_call(
        functools.partial(kernel, sizes, extents),
        out_shape=(
            jax.ShapeDtypeStruct((kinds * patches, lanes), F32),
            jax.ShapeDtypeStruct((patches, lanes), F32),
        ),
        in_specs=[pl.BlockSpec(memory_space=pltpu.HBM)] + [vmem] * 8 + [smem] * 2,
        out_specs=(vmem, vmem),
        scratch_shapes=[
            pltpu.VMEM((kinds * patches, lanes), F32),
            pltpu.VMEM((patches,) + tile, F32),
            pltpu.VMEM((patches, photons, lanes), F32),
            pltpu.VMEM((patches, photons, lanes), F32),
            pltpu.VMEM((patches,) + tile, F32),
            pltpu.VMEM((patches,) + tile, F32),
            pltpu.VMEM((north,) + tile, F32),
            pltpu.VMEM((north,) + tile, F32),
            pltpu.VMEM(tile, F32),
            pltpu.VMEM(tile, F32),
            pltpu.VMEM((levels + 1, east) + tile, F32),
            pltpu.VMEM((levels, east) + tile, F32),
            pltpu.VMEM((east,) + tile, F32),
            pltpu.VMEM((east,) + tile, F32),
            pltpu.VMEM((patches, photons, lanes), F32),
            pltpu.VMEM((patches, photons, lanes), F32),
            pltpu.VMEM((patches, photons, lanes), F32),
            pltpu.VMEM((patches, 2 * kinds + 16, lanes), F32),
            pltpu.VMEM((patches, lanes), F32),
            pltpu.VMEM((patches, lanes), F32),
            pltpu.VMEM((patches, lanes), F32),
            pltpu.VMEM((patches, lanes), F32),
            pltpu.VMEM((patches, lanes), F32),
            pltpu.VMEM((patches,) + tile, F32),
            pltpu.VMEM((2 * east,) + tile, F32),
            pltpu.VMEM((2 * east,) + tile, F32),
            pltpu.VMEM(tile, F32),
            pltpu.VMEM(tile, F32),
            pltpu.VMEM((slots,) + tile, F32),
            pltpu.VMEM((8, lanes), F32),
            pltpu.VMEM((photons, 2 * kinds), BF16),
            pltpu.VMEM((photons, 2 * kinds), BF16),
            pltpu.VMEM((photons, lanes), F32),
            pltpu.VMEM((reactions + two + 16, 2 * kinds), BF16),
            pltpu.VMEM((2 * kinds + 16, 2 * photons), BF16),
            pltpu.VMEM((2 * kinds + 16, 2 * two), BF16),
            pltpu.VMEM((2 * lanes, 2 * lanes), BF16),
            pltpu.VMEM((two, lanes), F32),
            pltpu.VMEM((two, lanes), F32),
            DMA((1,)),
            DMA((6,)),
            DMA((6,)),
            DMA((levels, east)),
            DMA((levels, east)),
            DMA((east,)),
            DMA((east,)),
            DMA((east,)),
            DMA((east,)),
            DMA((east,)),
            DMA((east,)),
            DMA((1,)),
            DMA((1,)),
        ],
        compiler_params=pltpu.CompilerParams(
            collective_id=0, has_side_effects=True, vmem_limit_bytes=48 << 20
        ),
    )(
        number_densities.reshape(kinds * patches, lanes),
        kinetic_kelvin.reshape(patches, lanes),
        flow_vector.reshape(3 * patches, lanes),
        opacity_area.T,
        arrhenius_coefficient.reshape(1, two),
        arrhenius_barrier.reshape(1, two),
        exothermic_energy.reshape(1, reactions),
        jnp.concatenate([emission_loss, emission_loss]).reshape(1, 2 * kinds),
        participant_indices,
        illumination,
        demanding_patches.reshape(slots),
    )
    return out.reshape(number_densities.shape), warm.reshape(kinetic_kelvin.shape)


def solution(mesh):
    cells = P(None, "gx", "gy", "gz")
    return jax.shard_map(
        functools.partial(shards, mesh.shape["gx"], mesh.shape["gy"], mesh.shape["gz"]),
        mesh=mesh,
        in_specs=(
            cells,
            P("gx", "gy", "gz"),
            cells,
            P(),
            P(),
            P(),
            P(),
            P(),
            P(),
            P(),
            P("gx", "gy", "gz", None),
        ),
        out_specs=(cells, P("gx", "gy", "gz")),
        check_vma=False,
    )
```

```python
import functools

import jax
import jax.numpy as jnp
from jax import lax
from jax.experimental import pallas as pl
from jax.experimental.pallas import tpu as pltpu
from jax.sharding import PartitionSpec as P

NSUB = 8
COURANT = 0.25
MESH = pl.DeviceIdType.MESH
F32 = jnp.float32
BF16 = jnp.bfloat16


def halves(x):
    high = x.astype(BF16)
    return high, (x - high.astype(F32)).astype(BF16)


def stacked(x):
    high, low = halves(x)
    return jnp.concatenate([high, low], axis=0)


def dot(a, b):
    return jnp.dot(a, b, preferred_element_type=F32)


def kernel(
    sizes,
    extents,
    n_ref,
    t_ref,
    flow_ref,
    opacity_ref,
    coef_ref,
    barrier_ref,
    energy_ref,
    emission_ref,
    part_ref,
    illum_ref,
    patch_ref,
    out_ref,
    warm_ref,
    tiles,
    depth,
    photo,
    chem,
    acc,
    xsum,
    xother,
    zsum,
    zother,
    scan,
    scan_in,
    below,
    above,
    ey_low,
    ey_up,
    first_a,
    first_pc,
    first_cool,
    flow_x,
    flow_l,
    flow_r,
    flow_z,
    halo_x,
    halo_l,
    halo_r,
    zpack,
    halo_z,
    hard_n,
    hard_t,
    op_hi,
    op_lo,
    pick,
    gather_mat,
    tally_p,
    tally_t,
    tri,
    coef_b,
    barr_b,
    sem_first_s,
    sem_first_r,
    sem_scan_s,
    sem_scan_r,
    sem_x_s,
    sem_x_r,
    sem_l_s,
    sem_l_r,
    sem_rt_s,
    sem_rt_r,
    sem_z_s,
    sem_z_r,
):
    kinds, east, north, lanes, photons, reactions, slots, ngy, levels = sizes
    patches = east * north
    gx, gy, gz = lax.axis_index("gx"), lax.axis_index("gy"), lax.axis_index("gz")
    peer_x = (1 - gx, gy, gz)
    peer_z = (gx, gy, 1 - gz)
    left = (gx, lax.rem(gy + ngy - 1, ngy), gz)
    right = (gx, lax.rem(gy + 1, ngy), gz)
    bits = [lax.rem(gy // (1 << k), 2) for k in range(levels)]
    partners = [(gx, gy + (1 << k) * (1 - 2 * bits[k]), gz) for k in range(levels)]

    entry = pltpu.get_barrier_semaphore()
    peers = [peer_x, peer_z] + partners
    for peer in peers:
        pl.semaphore_signal(entry, inc=1, device_id=peer, device_id_type=MESH)

    def send(src, dst, ssem, rsem, to):
        return pltpu.make_async_remote_copy(
            src_ref=src,
            dst_ref=dst,
            send_sem=ssem,
            recv_sem=rsem,
            device_id=to,
            device_id_type=MESH,
        )

    lane = lax.broadcasted_iota(jnp.int32, (kinds, lanes), 1)


    xs = [None] * north
    zt = jnp.zeros((kinds, lanes), F32)
    for i in range(east):
        row = None
        for j in range(north):
            t = i * north + j
            v = n_ref[pl.ds(t, kinds, stride=patches), :]
            tiles[t] = v
            row = v if row is None else row + v
            xs[j] = v if xs[j] is None else xs[j] + v
            zt = jnp.where(lane == t, jnp.sum(v, axis=1, keepdims=True), zt)
        scan[0, i] = row
    for j in range(north):
        xsum[j] = xs[j]
    zsum[...] = zt

    pl.semaphore_wait(entry, len(peers))

    def scan_copy(k, i):
        return send(
            scan.at[k, i], scan_in.at[k, i], sem_scan_s.at[k, i], sem_scan_r.at[k, i], partners[k]
        )

    for i in range(east):
        scan_copy(0, i).start()
    first = [
        send(xsum, xother, sem_first_s.at[0], sem_first_r.at[0], peer_x),
        send(zsum, zother, sem_first_s.at[1], sem_first_r.at[1], peer_z),
        send(
            flow_ref.at[pl.ds(0, patches)], flow_x, sem_first_s.at[2], sem_first_r.at[2], peer_x
        ),
        send(
            flow_ref.at[pl.ds(2 * patches, patches)],
            flow_z,
            sem_first_s.at[5],
            sem_first_r.at[5],
            peer_z,
        ),
    ]
    for copy in first:
        copy.start()

    op = opacity_ref[...].T
    op = jnp.concatenate([op, op], axis=1)
    op_high, op_low = halves(op)
    op_hi[...] = op_high
    lane_p = lax.broadcasted_iota(jnp.int32, op.shape, 1)
    op_lo[...] = jnp.where(lane_p < kinds, op_low.astype(F32), 0.0).astype(BF16)

    twice = lax.broadcasted_iota(jnp.int32, (2 * kinds, reactions), 0)
    twice = jnp.where(twice >= kinds, twice - kinds, twice)
    hot_a = (twice == part_ref[0:1, :]).astype(F32)
    gather_mat[0:reactions, :] = hot_a.T.astype(BF16)
    two = reactions - photons
    hot_b = (twice[:, photons:] == part_ref[1:2, photons:]).astype(F32)
    gather_mat[reactions : reactions + two, :] = hot_b.T.astype(BF16)
    extra = lax.broadcasted_iota(jnp.int32, (16, 2 * kinds), 0)
    q_high, q_low = halves(emission_ref[...])
    gather_mat[reactions + two :, :] = jnp.where(
        extra == 0, q_high.astype(F32), jnp.where(extra == 1, q_low.astype(F32), 0.0)
    ).astype(BF16)

    species = lax.broadcasted_iota(jnp.int32, (kinds, reactions), 0)
    which = lax.broadcasted_iota(jnp.int32, (kinds, reactions), 1)
    made = (species == part_ref[2:3, :]).astype(F32) + (species == part_ref[3:4, :]).astype(F32)
    used_up = (species == part_ref[0:1, :]).astype(F32) + jnp.where(
        which >= photons, (species == part_ref[1:2, :]).astype(F32), 0.0
    )
    extra = lax.broadcasted_iota(jnp.int32, (16, reactions), 0)
    e_high, e_low = halves(energy_ref[...])
    heats = jnp.where(
        extra == 0, e_high.astype(F32), jnp.where(extra == 1, e_low.astype(F32), 0.0)
    )
    tally = jnp.concatenate([made, used_up, heats], axis=0)
    tally_p[...] = jnp.concatenate([tally[:, :photons]] * 2, axis=1).astype(BF16)
    tally_t[...] = jnp.concatenate([tally[:, photons:]] * 2, axis=1).astype(BF16)

    source = lax.broadcasted_iota(jnp.int32, (2 * lanes, 2 * lanes), 0)
    source = jnp.where(source >= lanes, source - lanes, source)
    target = lax.broadcasted_iota(jnp.int32, (2 * lanes, 2 * lanes), 1)
    tri[...] = jnp.where(
        source < target, 1.0, jnp.where(source == target, 0.5, 0.0)
    ).astype(BF16)

    coef_b[...] = jnp.broadcast_to(coef_ref[...], (lanes, two)).T
    barr_b[...] = jnp.broadcast_to(-barrier_ref[...], (lanes, two)).T

    def project(x):
        s = stacked(x)
        return dot(op_hi[...], s) + dot(op_lo[...], s)

    def depth_row(i, carry):
        x = jnp.concatenate([tiles[i * north + j] for j in range(north)], axis=1)
        m = project(x)
        for j in range(north):
            depth[i * north + j] = m[:, j * lanes : (j + 1) * lanes]
        return carry

    lax.fori_loop(0, east, depth_row, 0)

    def scan_step(k, i):
        bit = bits[k].astype(F32)
        scan_copy(k, i).wait_recv()
        got = scan_in[k, i]
        if k + 1 < levels:
            scan[k + 1, i] = scan[k, i] + got
            scan_copy(k + 1, i).start()
        if k == 0:
            below[i] = bit * got
            above[i] = (1.0 - bit) * got
        else:
            below[i] = below[i] + bit * got
            above[i] = above[i] + (1.0 - bit) * got

    def scan_chunk(k, i, carry):
        scan_step(k, i)
        return carry

    def y_lines(i, carry):
        ms = [depth[i * north + j] for j in range(north)]
        whole = ms[0]
        for m in ms[1:]:
            whole = whole + m
        run = None
        for j in range(north):
            low = 0.5 * ms[j] if run is None else run + 0.5 * ms[j]
            t = i * north + j
            ey_low[t] = illum_ref[2] * jnp.exp(low * (-1.0 / extents[1]))
            ey_up[t] = illum_ref[3] * jnp.exp((whole - low) * (-1.0 / extents[1]))
            run = ms[j] if run is None else run + ms[j]
        return carry

    high_x = gx.astype(F32)

    def x_lines(j, carry):
        other = project(xother[j])
        ms = [depth[i * north + j] for i in range(east)]
        whole = other
        for m in ms:
            whole = whole + m
        run = high_x * other
        for i in range(east):
            low = run + 0.5 * ms[i]
            up = whole - low
            photo[i * north + j] = illum_ref[0] * jnp.exp(
                low * (-1.0 / extents[0])
            ) + illum_ref[1] * jnp.exp(up * (-1.0 / extents[0]))
            run = run + ms[i]
        return carry

    high_z = gz.astype(F32)

    def z_row(i):
        parts = []
        for j in range(north):
            high, low_part = halves(depth[i * north + j])
            parts.append(jnp.concatenate([high, low_part], axis=1))
        both = dot(jnp.concatenate(parts, axis=0), tri[...])
        for j in range(north):
            t = i * north + j
            other = pick[:, t : t + 1]
            rows = slice(j * photons, (j + 1) * photons)
            low = both[rows, :lanes] + high_z * other
            up = both[rows, lanes:] + other - low
            photo[t] = photo[t] + (
                illum_ref[4] * jnp.exp(low * (-1.0 / extents[2]))
                + illum_ref[5] * jnp.exp(up * (-1.0 / extents[2]))
            )

    def two_body(ns, ts):
        g = dot(gather_mat[...], jnp.concatenate([stacked(n) for n in ns], axis=1))
        rates = []
        for q in range(len(ns)):
            c = slice(q * lanes, (q + 1) * lanes)
            speed = coef_b[...] * jnp.exp(barr_b[...] * (1.0 / ts[q]))
            rates.append(
                stacked(speed * g[photons:reactions, c] * g[reactions : reactions + two, c])
            )
        pc = dot(tally_t[...], jnp.concatenate(rates, axis=1))
        result = []
        for q in range(len(ns)):
            c = slice(q * lanes, (q + 1) * lanes)
            cool = (
                g[reactions + two : reactions + two + 1, c]
                + g[reactions + two + 1 : reactions + two + 2, c]
            )
            result.append((g[:photons, c], pc[:, c], cool))
        return result

    def finish(ns, ts, ps, halfway, h):
        rates = [stacked(p * half[0]) for p, half in zip(ps, halfway)]
        pc_all = dot(tally_p[...], jnp.concatenate(rates, axis=1))
        new_n, new_t = [], []
        for q in range(len(ns)):
            c = slice(q * lanes, (q + 1) * lanes)
            n = ns[q]
            pc = pc_all[:, c] + halfway[q][1]
            gained, used = pc[:kinds], pc[kinds : 2 * kinds]
            new_n.append((n + h * gained) * (n / (n + h * used)))
            heat = pc[2 * kinds : 2 * kinds + 1] + pc[2 * kinds + 1 : 2 * kinds + 2]
            new_t.append((ts[q] + h * heat) / (1.0 + h * halfway[q][2]))
        return new_n, new_t

    def first_row(i, carry):
        index = [i * north + j for j in range(north)]
        found = two_body([tiles[t] for t in index], [t_ref[pl.ds(t, 1), :] for t in index])
        for t, (a, pc, cool) in zip(index, found):
            first_a[t] = a
            first_pc[t] = pc
            first_cool[pl.ds(t, 1), :] = cool
        return carry

    def x_part():
        first[0].wait_recv()
        lax.fori_loop(0, north, x_lines, 0)
        first[1].wait_recv()
        pick[...] = project(zother[...])

    def z_part():
        for i in range(east):
            z_row(i)

    def y_part():
        lax.fori_loop(0, east, y_lines, 0)

    def first_part():
        lax.fori_loop(0, east, first_row, 0)

    pieces = [[y_part], [x_part], [first_part, z_part]]
    for k in range(levels):
        for piece in pieces[k] if k < len(pieces) else []:
            piece()
        lax.fori_loop(0, east, functools.partial(scan_chunk, k), 0)

    flow_y = [
        send(
            flow_ref.at[pl.ds(patches, patches)],
            flow_r,
            sem_first_s.at[3],
            sem_first_r.at[3],
            left,
        ),
        send(
            flow_ref.at[pl.ds(patches, patches)],
            flow_l,
            sem_first_s.at[4],
            sem_first_r.at[4],
            right,
        ),
    ]
    for copy in flow_y:
        copy.start()

    def y_join(i, carry):
        low = jnp.exp(project(below[i]) * (-1.0 / extents[1]))
        up = jnp.exp(project(above[i]) * (-1.0 / extents[1]))
        for j in range(north):
            t = i * north + j
            photo[t] = photo[t] + (ey_low[t] * low + ey_up[t] * up)
        return carry

    lax.fori_loop(0, east, y_join, 0)

    listed = [patch_ref[d] for d in range(slots)]
    chosen = [jnp.minimum(d, patches - 1) for d in listed]
    hard_p = lambda: [photo[chosen[d]] for d in range(slots)]

    def keep(ns, ts):
        for d in range(slots):
            hard_n[d] = ns[d]
            hard_t[pl.ds(d, 1), :] = ts[d]

    keep(
        *finish(
            [tiles[t] for t in chosen],
            [t_ref[pl.ds(t, 1), :] for t in chosen],
            hard_p(),
            [(first_a[t], first_pc[t], first_cool[pl.ds(t, 1), :]) for t in chosen],
            1.0 / NSUB,
        )
    )

    def substep(_, carry):
        ns = [hard_n[d] for d in range(slots)]
        ts = [hard_t[pl.ds(d, 1), :] for d in range(slots)]
        keep(*finish(ns, ts, hard_p(), two_body(ns, ts), 1.0 / NSUB))
        return carry

    lax.fori_loop(1, NSUB, substep, 0)

    def copy_left(i):
        return send(
            chem.at[pl.ds(i * north, 2)],
            halo_r.at[pl.ds(i * 2, 2)],
            sem_l_s.at[i],
            sem_l_r.at[i],
            left,
        )

    def copy_right(i):
        return send(
            chem.at[pl.ds(i * north + north - 2, 2)],
            halo_l.at[pl.ds(i * 2, 2)],
            sem_rt_s.at[i],
            sem_rt_r.at[i],
            right,
        )

    def copy_x(i):
        return send(
            chem.at[pl.ds(i * north, north)],
            halo_x.at[pl.ds(i * north, north)],
            sem_x_s.at[i],
            sem_x_r.at[i],
            peer_x,
        )

    def quiet_row(i, carry):
        index = [i * north + j for j in range(north)]
        ns = [tiles[t] for t in index]
        ts = [t_ref[pl.ds(t, 1), :] for t in index]
        ps = [photo[t] for t in index]
        halfway = [(first_a[t], first_pc[t], first_cool[pl.ds(t, 1), :]) for t in index]
        ns, ts = finish(ns, ts, ps, halfway, 1.0)
        for j in range(north):
            t = index[j]
            n, warm = ns[j], ts[j]
            for d in range(slots):
                n = jnp.where(jnp.full((kinds, lanes), listed[d] - t, jnp.int32) == 0, hard_n[d], n)
                warm = jnp.where(
                    jnp.full((1, lanes), listed[d] - t, jnp.int32) == 0,
                    hard_t[pl.ds(d, 1), :],
                    warm,
                )
            chem[t] = n
            warm_ref[pl.ds(t, 1), :] = warm
        copy_left(i).start()
        copy_right(i).start()
        copy_x(i).start()
        return carry

    lax.fori_loop(0, east, quiet_row, 0)

    packed = jnp.zeros((kinds, lanes), F32)
    for t in range(patches):
        rolled = pltpu.roll(chem[t], (4 * t + 2) % lanes, 1)
        packed = jnp.where(lane // 4 == t, rolled, packed)
    zpack[...] = packed
    zcopy = send(zpack, halo_z, sem_z_s.at[0], sem_z_r.at[0], peer_z)
    zcopy.start()

    for copy in first[2:] + flow_y:
        copy.wait_recv()

    def flux(face, behind2, behind, ahead, ahead2):
        return face * jnp.where(
            face > 0, 1.5 * behind - 0.5 * behind2, 1.5 * ahead - 0.5 * ahead2
        )

    def flow_row(ref, t):
        return ref[pl.ds(t, 1), :]

    for i in range(east):
        copy_x(i).wait_recv()

    def advect_x(j, carry):
        cells = [halo_x[(east - 2) * north + j], halo_x[(east - 1) * north + j]]
        cells += [chem[i * north + j] for i in range(east)]
        cells += [halo_x[j], halo_x[north + j]]
        speed = [flow_row(flow_x, (east - 1) * north + j)]
        speed += [flow_row(flow_ref, i * north + j) for i in range(east)]
        speed += [flow_row(flow_x, j)]
        before = None
        for f in range(east + 1):
            face = jnp.broadcast_to(0.5 * (speed[f] + speed[f + 1]), (kinds, lanes))
            now = flux(face, cells[f], cells[f + 1], cells[f + 2], cells[f + 3])
            if f > 0:
                acc[(f - 1) * north + j] = now - before
            before = now
        return carry

    lax.fori_loop(0, north, advect_x, 0)

    zcopy.wait_recv()
    lane1 = lax.broadcasted_iota(jnp.int32, (1, lanes), 1)

    def roll(x, amount):
        return pltpu.roll(x, amount % lanes, 1)

    hz = halo_z[...]
    for t in range(patches):
        u = chem[t]
        b1 = jnp.where(lane == 0, roll(hz, -(4 * t + 1)), roll(u, 1))
        b2 = jnp.where(lane < 2, roll(hz, -4 * t), roll(u, 2))
        a1 = jnp.where(lane == lanes - 1, roll(hz, lanes - 1 - (4 * t + 2)), roll(u, -1))
        a2 = jnp.where(lane >= lanes - 2, roll(hz, lanes - 2 - (4 * t + 2)), roll(u, -2))
        v = flow_row(flow_ref, 2 * patches + t)
        vp = flow_row(flow_z, t)
        lower = 0.5 * (jnp.where(lane1 == 0, roll(vp, 1), roll(v, 1)) + v)
        upper = 0.5 * (v + jnp.where(lane1 == lanes - 1, roll(vp, -1), roll(v, -1)))
        lower = jnp.broadcast_to(lower, (kinds, lanes))
        upper = jnp.broadcast_to(upper, (kinds, lanes))
        acc[t] = acc[t] + (flux(upper, b1, u, a1, a2) - flux(lower, b2, b1, u, a1))

    for i in range(east):
        copy_left(i).wait_recv()
        copy_right(i).wait_recv()
        cells = [halo_l[2 * i], halo_l[2 * i + 1]]
        cells += [chem[i * north + j] for j in range(north)]
        cells += [halo_r[2 * i], halo_r[2 * i + 1]]
        speed = [flow_row(flow_l, i * north + north - 1)]
        speed += [flow_row(flow_ref, patches + i * north + j) for j in range(north)]
        speed += [flow_row(flow_r, i * north)]
        before = None
        for f in range(north + 1):
            face = jnp.broadcast_to(0.5 * (speed[f] + speed[f + 1]), (kinds, lanes))
            now = flux(face, cells[f], cells[f + 1], cells[f + 2], cells[f + 3])
            if f > 0:
                t = i * north + f - 1
                change = acc[t] + (now - before)
                out_ref[pl.ds(t, kinds, stride=patches), :] = chem[t] - COURANT * change
            before = now

    for copy in first + flow_y:
        copy.wait_send()
    for k in range(levels):
        for i in range(east):
            scan_copy(k, i).wait_send()
    for i in range(east):
        copy_left(i).wait_send()
        copy_right(i).wait_send()
        copy_x(i).wait_send()
    zcopy.wait_send()


def shards(
    ngx,
    ngy,
    ngz,
    number_densities,
    kinetic_kelvin,
    flow_vector,
    opacity_area,
    illumination,
    arrhenius_coefficient,
    arrhenius_barrier,
    exothermic_energy,
    emission_loss,
    participant_indices,
    demanding_patches,
):
    kinds, east, north, lanes = number_densities.shape
    photons = opacity_area.shape[0]
    reactions = participant_indices.shape[1]
    two = reactions - photons
    slots = demanding_patches.shape[-1]
    patches = east * north
    levels = ngy.bit_length() - 1
    assert ngx == 2 and ngz == 2 and ngy == 1 << levels
    sizes = (kinds, east, north, lanes, photons, reactions, slots, ngy, levels)
    extents = (float(east * ngx), float(north * ngy), float(lanes * ngz))
    vmem = pl.BlockSpec(memory_space=pltpu.VMEM)
    smem = pl.BlockSpec(memory_space=pltpu.SMEM)
    tile = (kinds, lanes)
    DMA = pltpu.SemaphoreType.DMA
    out, warm = pl.pallas_call(
        functools.partial(kernel, sizes, extents),
        out_shape=(
            jax.ShapeDtypeStruct((kinds * patches, lanes), F32),
            jax.ShapeDtypeStruct((patches, lanes), F32),
        ),
        in_specs=[vmem] * 9 + [smem] * 2,
        out_specs=(vmem, vmem),
        scratch_shapes=[
            pltpu.VMEM((patches,) + tile, F32),
            pltpu.VMEM((patches, photons, lanes), F32),
            pltpu.VMEM((patches, photons, lanes), F32),
            pltpu.VMEM((patches,) + tile, F32),
            pltpu.VMEM((patches,) + tile, F32),
            pltpu.VMEM((north,) + tile, F32),
            pltpu.VMEM((north,) + tile, F32),
            pltpu.VMEM(tile, F32),
            pltpu.VMEM(tile, F32),
            pltpu.VMEM((levels + 1, east) + tile, F32),
            pltpu.VMEM((levels, east) + tile, F32),
            pltpu.VMEM((east,) + tile, F32),
            pltpu.VMEM((east,) + tile, F32),
            pltpu.VMEM((patches, photons, lanes), F32),
            pltpu.VMEM((patches, photons, lanes), F32),
            pltpu.VMEM((patches, photons, lanes), F32),
            pltpu.VMEM((patches, 2 * kinds + 16, lanes), F32),
            pltpu.VMEM((patches, lanes), F32),
            pltpu.VMEM((patches, lanes), F32),
            pltpu.VMEM((patches, lanes), F32),
            pltpu.VMEM((patches, lanes), F32),
            pltpu.VMEM((patches, lanes), F32),
            pltpu.VMEM((patches,) + tile, F32),
            pltpu.VMEM((2 * east,) + tile, F32),
            pltpu.VMEM((2 * east,) + tile, F32),
            pltpu.VMEM(tile, F32),
            pltpu.VMEM(tile, F32),
            pltpu.VMEM((slots,) + tile, F32),
            pltpu.VMEM((8, lanes), F32),
            pltpu.VMEM((photons, 2 * kinds), BF16),
            pltpu.VMEM((photons, 2 * kinds), BF16),
            pltpu.VMEM((photons, lanes), F32),
            pltpu.VMEM((reactions + two + 16, 2 * kinds), BF16),
            pltpu.VMEM((2 * kinds + 16, 2 * photons), BF16),
            pltpu.VMEM((2 * kinds + 16, 2 * two), BF16),
            pltpu.VMEM((2 * lanes, 2 * lanes), BF16),
            pltpu.VMEM((two, lanes), F32),
            pltpu.VMEM((two, lanes), F32),
            DMA((6,)),
            DMA((6,)),
            DMA((levels, east)),
            DMA((levels, east)),
            DMA((east,)),
            DMA((east,)),
            DMA((east,)),
            DMA((east,)),
            DMA((east,)),
            DMA((east,)),
            DMA((1,)),
            DMA((1,)),
        ],
        compiler_params=pltpu.CompilerParams(
            collective_id=0, has_side_effects=True, vmem_limit_bytes=48 << 20
        ),
    )(
        number_densities.reshape(kinds * patches, lanes),
        kinetic_kelvin.reshape(patches, lanes),
        flow_vector.reshape(3 * patches, lanes),
        opacity_area.T,
        arrhenius_coefficient.reshape(1, two),
        arrhenius_barrier.reshape(1, two),
        exothermic_energy.reshape(1, reactions),
        jnp.concatenate([emission_loss, emission_loss]).reshape(1, 2 * kinds),
        participant_indices,
        illumination,
        demanding_patches.reshape(slots),
    )
    return out.reshape(number_densities.shape), warm.reshape(kinetic_kelvin.shape)


def solution(mesh):
    cells = P(None, "gx", "gy", "gz")
    return jax.shard_map(
        functools.partial(shards, mesh.shape["gx"], mesh.shape["gy"], mesh.shape["gz"]),
        mesh=mesh,
        in_specs=(
            cells,
            P("gx", "gy", "gz"),
            cells,
            P(),
            P(),
            P(),
            P(),
            P(),
            P(),
            P(),
            P("gx", "gy", "gz", None),
        ),
        out_specs=(cells, P("gx", "gy", "gz")),
        check_vma=False,
    )
```
